256 devices in a mesh: grp: 32 (over y, z), band: 8 (over x, core).
Axes of the slice: x: 4, y: 4, z: 8, core: 2. Of those that a mesh axis runs over, the one named last changes fastest.
Arguments:
- spectra: bfloat16 [2, 32, 64, 4096], P(None, None, 'band', 'grp'), may hold values from -140 to 140, as said below
- tile_band: int32 [32, 32], P('grp'), may hold values from 0 to 8, as said below
Outputs:
- gathers: bfloat16 [32, 8, 64, 128, 256], P('grp', 'band')
The draws below stay inside these ranges and needn't reach their ends.
Inputs may be any that keep to these rules, and one draw needn't show every extreme that they name: `spectra`: entries are of order one times a scale of each window and channel. `tile_band`: entry (i, j) is |i - j| * 8 // 32, or 8 where the pair is not stacked; it is 8 where i = j, and never 8 where |i - j| = 1.
All inputs are finite; a program needn't handle non-finite values.
Results may differ from the reference program's by a relative error of at most 0.0064.
Values may be sent and summed in bfloat16 or wider, within the bound.
No kernel may reach another device: no remote copies, remote signals or barrier semaphores. Data moves between devices by JAX's collectives and lax.ppermute only.
A program may use at most 64 MiB of HBM per device.

```python
import jax
import jax.numpy as jnp
from jax import lax

TILE = 128
WINDOWS = 32
BLOCKS = 32
BANDS = 8
BINS = 64
CHANNELS = 4096


def draw_spectra(key, part):
    entry_key = jax.random.fold_in(key, 11)
    scale_key = jax.random.fold_in(key, 23)
    shape = (2, WINDOWS, BINS, CHANNELS)
    entries = jnp.clip(jax.random.normal(entry_key, shape, jnp.float32), -5.0, 5.0)
    levels = jax.random.uniform(scale_key, (WINDOWS, CHANNELS), jnp.float32, 0.0, jnp.log(10.0))
    rising = jnp.sqrt(3.0 ** (jnp.arange(BINS, dtype=jnp.float32) / max(BINS - 1, 1)))
    return (entries * jnp.exp(levels)[None, :, None, :] * rising[None, None, :, None]).astype(jnp.bfloat16)


def draw_tile_band(key, part):
    rows = jnp.arange(BLOCKS, dtype=jnp.int32)[:, None]
    cols = jnp.arange(BLOCKS, dtype=jnp.int32)[None, :]
    offset = jnp.abs(rows - cols)
    banded = offset * BANDS // BLOCKS
    dropped = (jax.random.randint(jax.random.fold_in(key, 5), (BLOCKS, BLOCKS), 0, 4) == 0) & (offset >= 2)
    return jnp.where((offset == 0) | dropped, BANDS, banded).astype(jnp.int32)


def setup_inputs(seed: int = 0) -> dict:
    key_of = jax.random.split(jax.random.key(seed), 3)
    spectra = draw_spectra(jax.random.fold_in(key_of[2], 71), 0)
    tile_band = draw_tile_band(jax.random.fold_in(key_of[2], 71), 0)
    return dict(spectra=spectra, tile_band=tile_band)


def reference(spectra, tile_band):
    values = spectra.astype(jnp.float32)
    power = lax.optimization_barrier(jnp.sum(values * values, axis=(0, 2)))
    white = (values * lax.rsqrt(power / BINS + 1e-05)[None, :, None, :]).astype(jnp.bfloat16)
    selector = (tile_band[:, None, :] == jnp.arange(BANDS, dtype=jnp.int32)[None, :, None]).astype(jnp.float32)
    counts = lax.optimization_barrier(jnp.sum(selector, axis=2))
    blocks_view = white.astype(jnp.float32).reshape(2, WINDOWS, BINS, BLOCKS, TILE)
    own_all = jnp.moveaxis(blocks_view, 3, 0)

    def one_source(inputs):
        row, weights, own = inputs
        partner = jnp.einsum('kn,pwfnc->kpwfc', row, blocks_view, precision=lax.Precision.HIGHEST)
        partner = lax.optimization_barrier(partner.astype(jnp.bfloat16)).astype(jnp.float32)
        real_part = partner[:, 0]
        imag_part = partner[:, 1]
        paired = jnp.stack([jnp.stack([real_part, imag_part], axis=3), jnp.stack([imag_part, -real_part], axis=3)], axis=1)
        gram = jnp.einsum('pwfa,kpwfqb->kfaqb', own, paired, precision=lax.Precision.HIGHEST)
        gram = gram.reshape(BANDS, BINS, TILE, 2 * TILE)
        return (gram / jnp.maximum(weights, 1.0)[:, None, None, None]).astype(jnp.bfloat16)
    return lax.map(one_source, (selector, counts, own_all))
```

```python
import jax
import jax.numpy as jnp
from jax import lax
from jax.sharding import PartitionSpec as P

Y, Z, X, C = 4, 8, 4, 2
ROWS = ("grp", "band")
SLOTS = 3


def shift(value, dy=0, dz=0, dx=0, dc=0):
    pairs = []
    for y in range(Y):
        for z in range(Z):
            for x in range(X):
                for c in range(C):
                    source = ((y * Z + z) * X + x) * C + c
                    target = (((y + dy) % Y * Z + (z + dz) % Z) * X + (x + dx) % X) * C + (c + dc) % C
                    pairs.append((source, target))
    return lax.ppermute(value, ROWS, pairs)


def by_distance(pieces, axis_index, size):
    stacked = jnp.stack(pieces, axis=0)
    order = (axis_index - jnp.arange(size)) % size
    return stacked, order


def local(spectra, tile_band):
    _, windows, bins, tile = spectra.shape
    grp = lax.axis_index("grp")
    band = lax.axis_index("band")
    y, z = grp // Z, grp % Z
    bands = lax.axis_size("band")

    rows = [tile_band] + [shift(tile_band, dy=d) for d in range(1, Y)]

    values = spectra.astype(jnp.float32)
    power = jnp.sum(values * values, axis=(0, 2))
    power = power + shift(power, dc=1)
    power = power + shift(power, dx=1) + shift(power, dx=2) + shift(power, dx=3)
    factor = lax.rsqrt(power / (bins * bands) + 1e-05)
    white = (values * factor[None, :, None, :]).astype(jnp.bfloat16)
    white = jnp.transpose(white, (2, 0, 1, 3))

    ahead = {0: white}
    for d in (2, -2, 1, -1):
        ahead[d] = shift(white, dz=-d)
    ahead[3] = shift(ahead[2], dz=-1)
    ahead[-3] = shift(ahead[-2], dz=1)
    ahead[4] = shift(ahead[2], dz=-2)

    mine = [white] + [shift(white, dx=d) for d in range(1, X)]
    mine = jnp.stack(mine, axis=0)
    other = shift(mine, dc=1)

    offsets = jnp.array([0, 1, 2, 3, 4, -1, -2, -3])
    blocks = jnp.stack([ahead[d] for d in (0, 1, 2, 3, 4, -1, -2, -3)], axis=0)
    held = (z + offsets) % Z

    def first_band(target_row, source_row):
        distance = 8 * (target_row - source_row) + z
        below = (distance - 7) // 4
        above = (-distance) // 4
        return jnp.where(target_row > source_row, below, jnp.where(target_row < source_row, above, 0))

    def sums(target_row, tb):
        part = jnp.take(tb[0].reshape(Y, Z), y, axis=0)
        part = jnp.take(part, held)
        first = first_band(target_row, y)
        return (part[None, :] == first + jnp.arange(SLOTS)[:, None]).astype(jnp.bfloat16)

    picks = jnp.concatenate([sums((y - d) % Y, rows[d]) for d in range(Y)], axis=0)
    partial = jnp.einsum("rn,nfpwc->rfpwc", picks, blocks, preferred_element_type=jnp.float32)
    partial = partial.astype(jnp.bfloat16).reshape(Y, SLOTS, bins, 2, windows, tile)
    arrived = [partial[0]] + [shift(partial[d], dy=-d) for d in range(1, Y)]
    slots = jnp.concatenate(arrived, axis=0)
    slot_band = jnp.concatenate([first_band(y, (y + d) % Y) + jnp.arange(SLOTS) for d in range(Y)])

    owners = jnp.stack(
        [((band // C + dx) % X) * C + (band % C + dc) % C for dx in range(X) for dc in range(C)]
    )
    place = (slot_band[None, :] == owners[:, None]).astype(jnp.bfloat16)
    partner = jnp.einsum("kr,rfpwc->kfpwc", place, slots, preferred_element_type=jnp.float32)
    partner = partner.astype(jnp.bfloat16)
    theirs = []
    for dx in range(X):
        for dc in range(C):
            at = dx * C + dc
            theirs.append(partner[0] if at == 0 else shift(partner[at], dx=dx, dc=dc))
    stacked = jnp.stack(theirs, axis=0)
    index = jnp.arange(bands)
    steps_x = (band // C - index // C) % X
    steps_c = (band % C - index % C) % C
    theirs = jnp.take(stacked, steps_x * C + steps_c, axis=0).reshape(bands * bins, 2, windows, tile)
    both = jnp.stack([mine, other], axis=1).reshape(bands, bins, 2, windows, tile)
    own = jnp.take(both, steps_x * C + steps_c, axis=0).reshape(bands * bins, 2, windows, tile)

    turned = jnp.stack([theirs[:, 1], -theirs[:, 0]], axis=1)
    paired = jnp.concatenate([theirs, turned], axis=3)
    gram = jnp.einsum("fpwa,fpwb->fab", own, paired, preferred_element_type=jnp.float32)
    count = jnp.sum((tile_band[0] == band).astype(jnp.float32))
    out = (gram / jnp.maximum(count, 1.0)).astype(jnp.bfloat16)
    return out[None, None]


def solution(mesh):
    return jax.shard_map(
        local,
        mesh=mesh,
        in_specs=(P(None, None, "band", "grp"), P("grp", None)),
        out_specs=P("grp", "band", None, None, None),
        check_vma=False,
    )
```

```python
import jax
import jax.numpy as jnp
from jax import lax
from jax.experimental import pallas as pl
from jax.experimental.pallas import tpu as pltpu
from jax.sharding import PartitionSpec as P

Y, Z, X, C = 4, 8, 4, 2
ROWS = ("grp", "band")
SLOTS = 3
AHEAD = (0, 1, 2, 3, 4, -1, -2, -3)
VMEM = pl.BlockSpec(memory_space=pltpu.VMEM)
SMEM = pl.BlockSpec(memory_space=pltpu.SMEM)
ANY = pl.BlockSpec(memory_space=pl.ANY)


def shift(value, dy=0, dz=0, dx=0, dc=0):
    pairs = []
    for y in range(Y):
        for z in range(Z):
            for x in range(X):
                for c in range(C):
                    source = ((y * Z + z) * X + x) * C + c
                    target = (((y + dy) % Y * Z + (z + dz) % Z) * X + (x + dx) % X) * C + (c + dc) % C
                    pairs.append((source, target))
    return lax.ppermute(value, ROWS, pairs)


def first_band(target_row, source_row, z):
    distance = Z * (target_row - source_row) + z
    low = jnp.where(target_row > source_row, distance - (Z - 1), -distance)
    return jnp.where(target_row == source_row, 0, lax.shift_right_arithmetic(low, 2))


def partial_kernel(pos, *refs):
    rows, blocks, outs = refs[:Y], refs[Y : Y + Z], refs[Y + Z :]
    bins, _, windows, tile = blocks[0].shape
    y, z = pos[0], pos[1]
    high = SLOTS * windows
    lane = lax.broadcasted_iota(jnp.int32, (high, Z * windows), 1)
    line = lax.broadcasted_iota(jnp.int32, (high, Z * windows), 0)
    same = lane % windows == line % windows
    picks = []
    for d in range(Y):
        first = first_band(lax.rem(y - d + Y, Y), y, z)
        bands = jnp.full((high, Z * windows), -1, jnp.int32)
        for n, off in enumerate(AHEAD):
            bands = jnp.where(lane // windows == n, rows[d][0, y * Z + lax.rem(z + off + Z, Z)], bands)
        picks.append(jnp.where(same & (bands == first + line // windows), 1.0, 0.0).astype(jnp.bfloat16))
    picks = jnp.concatenate(picks, axis=0)
    for f in range(bins):
        both = [jnp.concatenate([b[f, p] for b in blocks], axis=0) for p in range(2)]
        sums = jnp.dot(picks, jnp.concatenate(both, axis=1), preferred_element_type=jnp.float32)
        sums = sums.astype(jnp.bfloat16)
        for d in range(Y):
            for s in range(SLOTS):
                at = (d * SLOTS + s) * windows
                for p in range(2):
                    outs[d][s, f, p] = sums[at : at + windows, p * tile : (p + 1) * tile]


def combine_kernel(pos, *refs):
    arrived, outs = refs[:Y], refs[Y:]
    _, bins, _, windows, tile = arrived[0].shape
    y, z, x, c = pos[0], pos[1], pos[2], pos[3]
    shape = (X * C * windows, Y * SLOTS * windows)
    lane = lax.broadcasted_iota(jnp.int32, shape, 1)
    line = lax.broadcasted_iota(jnp.int32, shape, 0)
    has = jnp.full(shape, -1, jnp.int32)
    wants = jnp.full(shape, -2, jnp.int32)
    for d in range(Y):
        first = first_band(y, lax.rem(y + d, Y), z)
        for s in range(SLOTS):
            has = jnp.where(lane // windows == d * SLOTS + s, first + s, has)
    for dx in range(X):
        for dc in range(C):
            owner = lax.rem(x + dx, X) * C + lax.rem(c + dc, C)
            wants = jnp.where(line // windows == dx * C + dc, owner, wants)
    place = jnp.where((lane % windows == line % windows) & (has == wants), 1.0, 0.0).astype(jnp.bfloat16)
    for f in range(bins):
        both = [jnp.concatenate([a[s, f, p] for a in arrived for s in range(SLOTS)], axis=0) for p in range(2)]
        sums = jnp.dot(place, jnp.concatenate(both, axis=1), preferred_element_type=jnp.float32)
        sums = sums.astype(jnp.bfloat16)
        for n in range(X * C):
            for p in range(2):
                outs[n][f, p] = sums[n * windows : (n + 1) * windows, p * tile : (p + 1) * tile]


def gram_kernel(pos, tile_band, *refs):
    many = X * C
    own, theirs, out, held, sems = refs[:many], refs[many : 2 * many], refs[-3], refs[-2], refs[-1]
    bins, _, windows, tile = own[0].shape
    x, c = pos[2], pos[3]
    band = x * C + c
    count = jnp.int32(0)
    for j in range(tile_band.shape[1]):
        count += jnp.where(tile_band[0, j] == band, 1, 0)
    scale = 1.0 / jnp.full((1, 2 * tile), jnp.maximum(count, 1), jnp.int32).astype(jnp.float32)
    copies = []
    for dx in range(X):
        for dc in range(C):
            n = dx * C + dc
            for f in range(bins):
                real, imag = theirs[n][f, 0], theirs[n][f, 1]
                paired = jnp.concatenate(
                    [jnp.concatenate([real, imag], axis=0), jnp.concatenate([imag, -real], axis=0)], axis=1
                )
                mine = jnp.concatenate([own[n][f, 0], own[n][f, 1]], axis=0)
                gram = lax.dot_general(
                    mine, paired, (((0,), (0,)), ((), ())), preferred_element_type=jnp.float32
                )
                held[n, f] = (gram * scale).astype(jnp.bfloat16)
            place = lax.rem(x - dx + X, X) * C + lax.rem(c - dc + C, C)
            copy = pltpu.make_async_copy(held.at[n], out.at[0, 0, pl.ds(place * bins, bins)], sems.at[n])
            copy.start()
            copies.append(copy)
    for copy in copies:
        copy.wait()


def local(spectra, tile_band):
    _, windows, bins, tile = spectra.shape
    grp = lax.axis_index("grp")
    band = lax.axis_index("band")
    bands = X * C
    pos = jnp.stack([grp // Z, grp % Z, band // C, band % C]).astype(jnp.int32)

    values = spectra.astype(jnp.float32)
    power = jnp.sum(values * values, axis=(0, 2))
    power = power + shift(power, dc=1)
    power = power + shift(power, dx=1) + shift(power, dx=2) + shift(power, dx=3)
    factor = lax.rsqrt(power / (bins * bands) + 1e-05)
    white = (values * factor[None, :, None, :]).astype(jnp.bfloat16)
    white = jnp.transpose(white, (2, 0, 1, 3))
    white, tile_late = lax.optimization_barrier((white, tile_band))

    ahead = {0: white}
    for d in (2, -2, 1, -1):
        ahead[d] = shift(white, dz=-d)
    ahead[3] = shift(ahead[2], dz=-1)
    ahead[-3] = shift(ahead[-2], dz=1)
    ahead[4] = shift(ahead[2], dz=-2)

    rows = [tile_late] + [shift(tile_late, dy=d) for d in range(1, Y)]

    mine = [white] + [shift(white, dx=d) for d in range(1, X)]
    own = []
    for piece in mine:
        own += [piece, shift(piece, dc=1)]

    slotted = jax.ShapeDtypeStruct((SLOTS, bins, 2, windows, tile), jnp.bfloat16)
    partial = pl.pallas_call(
        partial_kernel,
        out_shape=[slotted] * Y,
        in_specs=[SMEM] * (1 + Y) + [VMEM] * Z,
        out_specs=[VMEM] * Y,
        name="partial",
    )(pos, *rows, *(ahead[d] for d in AHEAD))
    arrived = [partial[0]] + [shift(partial[d], dy=-d) for d in range(1, Y)]

    block = jax.ShapeDtypeStruct((bins, 2, windows, tile), jnp.bfloat16)
    partner = pl.pallas_call(
        combine_kernel,
        out_shape=[block] * bands,
        in_specs=[SMEM] + [VMEM] * Y,
        out_specs=[VMEM] * bands,
        name="combine",
    )(pos, *arrived)
    theirs = [
        partner[dx * C + dc] if dx == dc == 0 else shift(partner[dx * C + dc], dx=dx, dc=dc)
        for dx in range(X)
        for dc in range(C)
    ]
    return pl.pallas_call(
        gram_kernel,
        out_shape=jax.ShapeDtypeStruct((1, 1, bands * bins, tile, 2 * tile), jnp.bfloat16),
        in_specs=[SMEM] * 2 + [VMEM] * (2 * bands),
        out_specs=ANY,
        scratch_shapes=[
            pltpu.VMEM((bands, bins, tile, 2 * tile), jnp.bfloat16),
            pltpu.SemaphoreType.DMA((bands,)),
        ],
        name="gram",
    )(pos, tile_band, *own, *theirs)


def solution(mesh):
    return jax.shard_map(
        local,
        mesh=mesh,
        in_specs=(P(None, None, "band", "grp"), P("grp", None)),
        out_specs=P("grp", "band", None, None, None),
        check_vma=False,
    )
```

```python
import functools

import jax
import jax.numpy as jnp
from jax import lax
from jax.experimental import pallas as pl
from jax.experimental.pallas import tpu as pltpu
from jax.sharding import PartitionSpec as P


Y, Z, X, C = 4, 8, 4, 2
ROWS = ("grp", "band")
SLOTS = 3
AHEAD = (0, 1, 2, 3, 4, -1, -2, -3)
VMEM = pl.BlockSpec(memory_space=pltpu.VMEM)
SMEM = pl.BlockSpec(memory_space=pltpu.SMEM)
ANY = pl.BlockSpec(memory_space=pl.ANY)


def shift(value, dy=0, dz=0, dx=0, dc=0):
    pairs = []
    for y in range(Y):
        for z in range(Z):
            for x in range(X):
                for c in range(C):
                    source = ((y * Z + z) * X + x) * C + c
                    target = (((y + dy) % Y * Z + (z + dz) % Z) * X + (x + dx) % X) * C + (c + dc) % C
                    pairs.append((source, target))
    return lax.ppermute(value, ROWS, pairs)


def spread(value):
    size = ((y, z, x, c) for y in range(Y) for z in range(Z) for x in range(X) for c in range(C))
    pairs = [(i, (((y + x) % Y * Z + z) * X + x) * C + c) for i, (y, z, x, c) in enumerate(size)]
    return lax.ppermute(value, ROWS, pairs)


def first_band(target_row, source_row, z):
    distance = Z * (target_row - source_row) + z
    low = jnp.where(target_row > source_row, distance - (Z - 1), -distance)
    return jnp.where(target_row == source_row, 0, lax.shift_right_arithmetic(low, 2))


def partial_kernel(pos, *refs):
    rows, blocks, outs = refs[0], refs[1 : 1 + Z], refs[1 + Z :]
    bins, _, windows, tile = blocks[0].shape
    y, z, x = pos[0], pos[1], pos[2]
    high = SLOTS * windows
    lane = lax.broadcasted_iota(jnp.int32, (high, Z * windows), 1)
    line = lax.broadcasted_iota(jnp.int32, (high, Z * windows), 0)
    same = lane % windows == line % windows
    picks = []
    for d in range(Y):
        first = first_band(lax.rem(y - d + Y, Y), y, z)
        row = lax.rem(x - d + X, X)
        bands = jnp.full((high, Z * windows), -1, jnp.int32)
        for n, off in enumerate(AHEAD):
            bands = jnp.where(lane // windows == n, rows[row, y * Z + lax.rem(z + off + Z, Z)], bands)
        picks.append(jnp.where(same & (bands == first + line // windows), 1.0, 0.0).astype(jnp.bfloat16))
    picks = jnp.concatenate(picks, axis=0)
    for f in range(bins):
        both = [jnp.concatenate([b[f, p] for b in blocks], axis=0) for p in range(2)]
        sums = jnp.dot(picks, jnp.concatenate(both, axis=1), preferred_element_type=jnp.float32)
        sums = sums.astype(jnp.bfloat16)
        for d in range(Y):
            for s in range(SLOTS):
                at = (d * SLOTS + s) * windows
                for p in range(2):
                    outs[d][s, f, p] = sums[at : at + windows, p * tile : (p + 1) * tile]


def combine_kernel(pos, *refs):
    arrived, outs = refs[:Y], refs[Y:]
    _, bins, _, windows, tile = arrived[0].shape
    y, z, x, c = pos[0], pos[1], pos[2], pos[3]
    shape = (X * C * windows, Y * SLOTS * windows)
    lane = lax.broadcasted_iota(jnp.int32, shape, 1)
    line = lax.broadcasted_iota(jnp.int32, shape, 0)
    has = jnp.full(shape, -1, jnp.int32)
    wants = jnp.full(shape, -2, jnp.int32)
    for d in range(Y):
        first = first_band(y, lax.rem(y + d, Y), z)
        for s in range(SLOTS):
            has = jnp.where(lane // windows == d * SLOTS + s, first + s, has)
    for dx in range(X):
        for dc in range(C):
            owner = lax.rem(x + dx, X) * C + lax.rem(c + dc, C)
            wants = jnp.where(line // windows == dx * C + dc, owner, wants)
    place = jnp.where((lane % windows == line % windows) & (has == wants), 1.0, 0.0).astype(jnp.bfloat16)
    for f in range(bins):
        both = [jnp.concatenate([a[s, f, p] for a in arrived for s in range(SLOTS)], axis=0) for p in range(2)]
        sums = jnp.dot(place, jnp.concatenate(both, axis=1), preferred_element_type=jnp.float32)
        sums = sums.astype(jnp.bfloat16)
        for n in range(X * C):
            for p in range(2):
                outs[n][f, p] = sums[n * windows : (n + 1) * windows, p * tile : (p + 1) * tile]


def gram_kernel(places, pos, tile_band, *refs):
    many = len(places)
    own, theirs, out, held, sems = refs[:many], refs[many : 2 * many], refs[-3], refs[-2], refs[-1]
    bins, _, _, tile = own[0].shape
    x, c = pos[2], pos[3]
    band = x * C + c
    count = jnp.int32(0)
    for j in range(tile_band.shape[1]):
        count += jnp.where(tile_band[0, j] == band, 1, 0)
    scale = 1.0 / jnp.full((1, 2 * tile), jnp.maximum(count, 1), jnp.int32).astype(jnp.float32)
    copies = []
    for n, (dx, dc) in enumerate(places):
        for f in range(bins):
            real, imag = theirs[n][f, 0], theirs[n][f, 1]
            paired = jnp.concatenate(
                [jnp.concatenate([real, imag], axis=0), jnp.concatenate([imag, -real], axis=0)], axis=1
            )
            mine = jnp.concatenate([own[n][f, 0], own[n][f, 1]], axis=0)
            gram = lax.dot_general(mine, paired, (((0,), (0,)), ((), ())), preferred_element_type=jnp.float32)
            held[n, f] = (gram * scale).astype(jnp.bfloat16)
        place = lax.rem(x - dx + X, X) * C + lax.rem(c - dc + C, C)
        copy = pltpu.make_async_copy(held.at[n], out.at[0, 0, pl.ds(place * bins, bins)], sems.at[n])
        copy.start()
        copies.append(copy)
    for copy in copies:
        copy.wait()


BATCHES = (((0, 0), (0, 1), (2, 0), (2, 1)), ((1, 0), (1, 1), (3, 0), (3, 1)))


def local(spectra, tile_band):
    _, windows, bins, tile = spectra.shape
    grp = lax.axis_index("grp")
    band = lax.axis_index("band")
    bands = X * C
    pos = jnp.stack([grp // Z, grp % Z, band // C, band % C]).astype(jnp.int32)

    row = spread(tile_band).astype(jnp.float32)
    values = spectra.astype(jnp.float32)
    power = jnp.sum(values * values, axis=(0, 2))
    power = power + shift(power, dc=1)
    sent = jnp.concatenate([power, jnp.pad(row, ((0, 7), (0, tile - row.shape[1])))], axis=0)
    crossed = {0: sent}
    for d in (2, 1, 3):
        crossed[d] = shift(sent, dx=d)
    rows = jnp.concatenate([crossed[d][windows : windows + 1, : row.shape[1]] for d in range(X)], axis=0)
    rows = rows.astype(jnp.int32)
    power = sum((crossed[d][:windows] for d in range(1, X)), crossed[0][:windows])
    factor = lax.rsqrt(power / (bins * bands) + 1e-05)
    white = (values * factor[None, :, None, :]).astype(jnp.bfloat16)
    white = jnp.transpose(white, (2, 0, 1, 3))

    ahead = {0: white}
    for d in (2, -2, 1, -1):
        ahead[d] = shift(white, dz=-d)
    ahead[3] = shift(ahead[2], dz=-1)
    ahead[-3] = shift(ahead[-2], dz=1)
    ahead[4] = shift(ahead[2], dz=-2)

    slotted = jax.ShapeDtypeStruct((SLOTS, bins, 2, windows, tile), jnp.bfloat16)
    partial = pl.pallas_call(
        partial_kernel,
        out_shape=[slotted] * Y,
        in_specs=[SMEM] * 2 + [VMEM] * Z,
        out_specs=[VMEM] * Y,
        compiler_params=pltpu.CompilerParams(vmem_limit_bytes=8 << 20),
        name="partial",
    )(pos, rows, *(ahead[d] for d in AHEAD))
    arrived = [shift(partial[d], dy=-d) if d else partial[d] for d in range(Y)]

    own = {(d, 0): shift(white, dx=d) if d else white for d in range(X)}
    for d in range(X):
        own[d, 1] = shift(own[d, 0], dc=1)

    block = jax.ShapeDtypeStruct((bins, 2, windows, tile), jnp.bfloat16)
    partner = pl.pallas_call(
        combine_kernel,
        out_shape=[block] * bands,
        in_specs=[SMEM] + [VMEM] * Y,
        out_specs=[VMEM] * bands,
        compiler_params=pltpu.CompilerParams(vmem_limit_bytes=8 << 20),
        name="combine",
    )(pos, *arrived)
    theirs = {}
    for dx in range(X):
        for dc in range(C):
            sent = partner[dx * C + dc]
            theirs[dx, dc] = shift(sent, dx=dx, dc=dc) if dx or dc else sent

    out = None
    for at, places in enumerate(BATCHES):
        operands = [own[n] for n in places] + [theirs[n] for n in places]
        out = pl.pallas_call(
            functools.partial(gram_kernel, places),
            out_shape=jax.ShapeDtypeStruct((1, 1, bands * bins, tile, 2 * tile), jnp.bfloat16),
            in_specs=[SMEM] * 2 + [VMEM] * len(operands) + [ANY] * (at > 0),
            out_specs=ANY,
            scratch_shapes=[
                pltpu.VMEM((len(places), bins, tile, 2 * tile), jnp.bfloat16),
                pltpu.SemaphoreType.DMA((len(places),)),
            ],
            input_output_aliases={2 + len(operands): 0} if at else {},
            compiler_params=pltpu.CompilerParams(vmem_limit_bytes=12 << 20),
        )(pos, tile_band, *operands, *([out] if at else []))
    return out


def solution(mesh):
    return jax.shard_map(
        local,
        mesh=mesh,
        in_specs=(P(None, None, "band", "grp"), P("grp", None)),
        out_specs=P("grp", "band", None, None, None),
        check_vma=False,
    )
```

```python
import functools

import jax
import jax.numpy as jnp
from jax import lax
from jax.experimental import pallas as pl
from jax.experimental.pallas import tpu as pltpu
from jax.sharding import PartitionSpec as P


Y, Z, X, C = 4, 8, 4, 2
ROWS = ("grp", "band")
SLOTS = 3
AHEAD = (0, 1, 2, 3, 4, -1, -2, -3)
VMEM = pl.BlockSpec(memory_space=pltpu.VMEM)
SMEM = pl.BlockSpec(memory_space=pltpu.SMEM)
ANY = pl.BlockSpec(memory_space=pl.ANY)


def shift(value, dy=0, dz=0, dx=0, dc=0):
    pairs = []
    for y in range(Y):
        for z in range(Z):
            for x in range(X):
                for c in range(C):
                    source = ((y * Z + z) * X + x) * C + c
                    target = (((y + dy) % Y * Z + (z + (-dz if c else dz)) % Z) * X + (x + dx) % X) * C + (c + dc) % C
                    pairs.append((source, target))
    return lax.ppermute(value, ROWS, pairs)


def spread(value):
    size = ((y, z, x, c) for y in range(Y) for z in range(Z) for x in range(X) for c in range(C))
    pairs = [(i, (((y + x) % Y * Z + z) * X + x) * C + c) for i, (y, z, x, c) in enumerate(size)]
    return lax.ppermute(value, ROWS, pairs)


def first_band(target_row, source_row, z):
    distance = Z * (target_row - source_row) + z
    low = jnp.where(target_row > source_row, distance - (Z - 1), -distance)
    return jnp.where(target_row == source_row, 0, lax.shift_right_arithmetic(low, 2))


def partial_kernel(pos, *refs):
    rows, blocks, outs = refs[0], refs[1 : 1 + Z], refs[1 + Z :]
    bins, _, windows, tile = blocks[0].shape
    y, z, x = pos[0], pos[1], pos[2]
    way = 1 - 2 * pos[3]
    high = SLOTS * windows
    lane = lax.broadcasted_iota(jnp.int32, (high, Z * windows), 1)
    line = lax.broadcasted_iota(jnp.int32, (high, Z * windows), 0)
    same = lane % windows == line % windows
    picks = []
    for d in range(Y):
        first = first_band(lax.rem(y - d + Y, Y), y, z)
        row = lax.rem(x - d + X, X)
        bands = jnp.full((high, Z * windows), -1, jnp.int32)
        for n, off in enumerate(AHEAD):
            bands = jnp.where(lane // windows == n, rows[row, y * Z + lax.rem(z + way * off + Z, Z)], bands)
        picks.append(jnp.where(same & (bands == first + line // windows), 1.0, 0.0).astype(jnp.bfloat16))
    picks = jnp.concatenate(picks, axis=0)
    for f in range(bins):
        both = [jnp.concatenate([b[f, p] for b in blocks], axis=0) for p in range(2)]
        sums = jnp.dot(picks, jnp.concatenate(both, axis=1), preferred_element_type=jnp.float32)
        sums = sums.astype(jnp.bfloat16)
        for d in range(Y):
            for s in range(SLOTS):
                at = (d * SLOTS + s) * windows
                for p in range(2):
                    outs[d][s, f, p] = sums[at : at + windows, p * tile : (p + 1) * tile]


def combine_kernel(pos, *refs):
    arrived, outs = refs[:Y], refs[Y:]
    _, bins, _, windows, tile = arrived[0].shape
    y, z, x, c = pos[0], pos[1], pos[2], pos[3]
    shape = (X * C * windows, Y * SLOTS * windows)
    lane = lax.broadcasted_iota(jnp.int32, shape, 1)
    line = lax.broadcasted_iota(jnp.int32, shape, 0)
    has = jnp.full(shape, -1, jnp.int32)
    wants = jnp.full(shape, -2, jnp.int32)
    for d in range(Y):
        first = first_band(y, lax.rem(y + d, Y), z)
        for s in range(SLOTS):
            has = jnp.where(lane // windows == d * SLOTS + s, first + s, has)
    for dx in range(X):
        for dc in range(C):
            owner = lax.rem(x + dx, X) * C + lax.rem(c + dc, C)
            wants = jnp.where(line // windows == dx * C + dc, owner, wants)
    place = jnp.where((lane % windows == line % windows) & (has == wants), 1.0, 0.0).astype(jnp.bfloat16)
    for f in range(bins):
        both = [jnp.concatenate([a[s, f, p] for a in arrived for s in range(SLOTS)], axis=0) for p in range(2)]
        sums = jnp.dot(place, jnp.concatenate(both, axis=1), preferred_element_type=jnp.float32)
        sums = sums.astype(jnp.bfloat16)
        for n in range(X * C):
            for p in range(2):
                outs[n][f, p] = sums[n * windows : (n + 1) * windows, p * tile : (p + 1) * tile]


def gram_kernel(places, pos, *refs):
    many = len(places)
    own, theirs, out, held, sems = refs[:many], refs[many : 2 * many], refs[-3], refs[-2], refs[-1]
    bins, _, _, tile = own[0].shape
    x, c = pos[2], pos[3]
    scale = 1.0 / jnp.full((1, 2 * tile), jnp.maximum(pos[4], 1), jnp.int32).astype(jnp.float32)
    copies = []
    for n, (dx, dc) in enumerate(places):
        for f in range(bins):
            real, imag = theirs[n][f, 0], theirs[n][f, 1]
            paired = jnp.concatenate(
                [jnp.concatenate([real, imag], axis=0), jnp.concatenate([imag, -real], axis=0)], axis=1
            )
            mine = jnp.concatenate([own[n][f, 0], own[n][f, 1]], axis=0)
            gram = lax.dot_general(mine, paired, (((0,), (0,)), ((), ())), preferred_element_type=jnp.float32)
            held[n, f] = (gram * scale).astype(jnp.bfloat16)
        place = lax.rem(x - dx + X, X) * C + lax.rem(c - dc + C, C)
        copy = pltpu.make_async_copy(held.at[n], out.at[0, 0, pl.ds(place * bins, bins)], sems.at[n])
        copy.start()
        copies.append(copy)
    for copy in copies:
        copy.wait()


BATCHES = (((0, 0), (0, 1), (2, 0), (2, 1), (1, 0), (1, 1)), ((3, 0), (3, 1)))


def local(spectra, tile_band):
    _, windows, bins, tile = spectra.shape
    grp = lax.axis_index("grp")
    band = lax.axis_index("band")
    bands = X * C
    count = jnp.sum((tile_band == band).astype(jnp.int32))
    pos = jnp.stack([grp // Z, grp % Z, band // C, band % C, count]).astype(jnp.int32)

    row = spread(tile_band).astype(jnp.float32)
    values = spectra.astype(jnp.float32)
    power = jnp.sum(values * values, axis=(0, 2))
    power = power + shift(power, dc=1)
    sent = jnp.concatenate([power, jnp.pad(row, ((0, 7), (0, tile - row.shape[1])))], axis=0)
    crossed = {0: sent}
    for d in (2, 1, 3):
        crossed[d] = shift(sent, dx=d)
    rows = jnp.concatenate([crossed[d][windows : windows + 1, : row.shape[1]] for d in range(X)], axis=0)
    rows = rows.astype(jnp.int32)
    power = sum((crossed[d][:windows] for d in range(1, X)), crossed[0][:windows])
    factor = lax.rsqrt(power / (bins * bands) + 1e-05)
    white = (values * factor[None, :, None, :]).astype(jnp.bfloat16)
    white = jnp.transpose(white, (2, 0, 1, 3))

    ahead = {0: white}
    for d in (2, -2, 1, -1):
        ahead[d] = shift(white, dz=-d)
    ahead[3] = shift(ahead[2], dz=-1)
    ahead[-3] = shift(ahead[-2], dz=1)
    ahead[4] = shift(ahead[2], dz=-2)

    slotted = jax.ShapeDtypeStruct((SLOTS, bins, 2, windows, tile), jnp.bfloat16)
    partial = pl.pallas_call(
        partial_kernel,
        out_shape=[slotted] * Y,
        in_specs=[SMEM] * 2 + [VMEM] * Z,
        out_specs=[VMEM] * Y,
        compiler_params=pltpu.CompilerParams(vmem_limit_bytes=8 << 20),
        name="partial",
    )(pos, rows, *(ahead[d] for d in AHEAD))
    arrived = [shift(partial[d], dy=-d) if d else partial[d] for d in range(Y)]

    own = {(d, 0): shift(white, dx=d) if d else white for d in range(X)}
    for d in range(X):
        own[d, 1] = shift(own[d, 0], dc=1)

    block = jax.ShapeDtypeStruct((bins, 2, windows, tile), jnp.bfloat16)
    partner = pl.pallas_call(
        combine_kernel,
        out_shape=[block] * bands,
        in_specs=[SMEM] + [VMEM] * Y,
        out_specs=[VMEM] * bands,
        compiler_params=pltpu.CompilerParams(vmem_limit_bytes=8 << 20),
        name="combine",
    )(pos, *arrived)
    theirs = {}
    for dx in range(X):
        for dc in range(C):
            sent = partner[dx * C + dc]
            theirs[dx, dc] = shift(sent, dx=dx, dc=dc) if dx or dc else sent

    out = None
    for at, places in enumerate(BATCHES):
        operands = [own[n] for n in places] + [theirs[n] for n in places]
        out = pl.pallas_call(
            functools.partial(gram_kernel, places),
            out_shape=jax.ShapeDtypeStruct((1, 1, bands * bins, tile, 2 * tile), jnp.bfloat16),
            in_specs=[SMEM] + [VMEM] * len(operands) + [ANY] * (at > 0),
            out_specs=ANY,
            scratch_shapes=[
                pltpu.VMEM((len(places), bins, tile, 2 * tile), jnp.bfloat16),
                pltpu.SemaphoreType.DMA((len(places),)),
            ],
            input_output_aliases={1 + len(operands): 0} if at else {},
            compiler_params=pltpu.CompilerParams(vmem_limit_bytes=12 << 20),
        )(pos, *operands, *([out] if at else []))
    return out


def solution(mesh):
    return jax.shard_map(
        local,
        mesh=mesh,
        in_specs=(P(None, None, "band", "grp"), P("grp", None)),
        out_specs=P("grp", "band", None, None, None),
        check_vma=False,
    )
```

```python
import functools

import jax
import jax.numpy as jnp
from jax import lax
from jax.experimental import pallas as pl
from jax.experimental.pallas import tpu as pltpu
from jax.sharding import PartitionSpec as P


Y, Z, X, C = 4, 8, 4, 2
ROWS = ("grp", "band")
SLOTS = 3
AHEAD = (0, 1, 2, 3, 4, -1, -2, -3)
VMEM = pl.BlockSpec(memory_space=pltpu.VMEM)
SMEM = pl.BlockSpec(memory_space=pltpu.SMEM)
ANY = pl.BlockSpec(memory_space=pl.ANY)


def shift(value, dy=0, dz=0, dx=0, dc=0):
    pairs = []
    for y in range(Y):
        for z in range(Z):
            for x in range(X):
                for c in range(C):
                    source = ((y * Z + z) * X + x) * C + c
                    target = (((y + dy) % Y * Z + (z + (-dz if c else dz)) % Z) * X + (x + dx) % X) * C + (c + dc) % C
                    pairs.append((source, target))
    return lax.ppermute(value, ROWS, pairs)


def spread(value):
    size = ((y, z, x, c) for y in range(Y) for z in range(Z) for x in range(X) for c in range(C))
    pairs = [(i, (((y + x) % Y * Z + z) * X + x) * C + c) for i, (y, z, x, c) in enumerate(size)]
    return lax.ppermute(value, ROWS, pairs)


def first_band(target_row, source_row, z):
    distance = Z * (target_row - source_row) + z
    low = jnp.where(target_row > source_row, distance - (Z - 1), -distance)
    return jnp.where(target_row == source_row, 0, lax.shift_right_arithmetic(low, 2))


def partial_kernel(pos, *refs):
    rows, blocks, outs = refs[0], refs[1 : 1 + Z], refs[1 + Z :]
    bins, _, windows, tile = blocks[0].shape
    y, z, x = pos[0], pos[1], pos[2]
    way = 1 - 2 * pos[3]
    high = SLOTS * windows
    lane = lax.broadcasted_iota(jnp.int32, (high, Z * windows), 1)
    line = lax.broadcasted_iota(jnp.int32, (high, Z * windows), 0)
    same = lane % windows == line % windows
    picks = []
    for d in range(Y):
        first = first_band(lax.rem(y - d + Y, Y), y, z)
        row = lax.rem(x - d + X, X)
        bands = jnp.full((high, Z * windows), -1, jnp.int32)
        for n, off in enumerate(AHEAD):
            bands = jnp.where(lane // windows == n, rows[row, y * Z + lax.rem(z + way * off + Z, Z)], bands)
        picks.append(jnp.where(same & (bands == first + line // windows), 1.0, 0.0).astype(jnp.bfloat16))
    picks = jnp.concatenate(picks, axis=0)
    for f in range(bins):
        both = [jnp.concatenate([b[f, p] for b in blocks], axis=0) for p in range(2)]
        sums = jnp.dot(picks, jnp.concatenate(both, axis=1), preferred_element_type=jnp.float32)
        sums = sums.astype(jnp.bfloat16)
        for d in range(Y):
            for s in range(SLOTS):
                at = (d * SLOTS + s) * windows
                for p in range(2):
                    outs[d][s, f, p] = sums[at : at + windows, p * tile : (p + 1) * tile]


def combine_kernel(pos, *refs):
    arrived, outs = (refs[:Y], refs[Y : 2 * Y]), refs[2 * Y :]
    _, bins, _, windows, tile = arrived[0][0].shape
    y, z, x, c = pos[0], pos[1], pos[2], pos[3]
    shape = (X * windows, Y * SLOTS * windows)
    lane = lax.broadcasted_iota(jnp.int32, shape, 1)
    line = lax.broadcasted_iota(jnp.int32, shape, 0)
    has = jnp.full(shape, -1, jnp.int32)
    wants = jnp.full(shape, -2, jnp.int32)
    for d in range(Y):
        first = first_band(y, lax.rem(y + d, Y), z)
        for s in range(SLOTS):
            has = jnp.where(lane // windows == d * SLOTS + s, first + s, has)
    for dx in range(X):
        wants = jnp.where(line // windows == dx, lax.rem(x + dx, X) * C + c, wants)
    place = jnp.where((lane % windows == line % windows) & (has == wants), 1.0, 0.0).astype(jnp.bfloat16)
    for q in range(C):
        for f in range(bins):
            both = [
                jnp.concatenate([a[s, f, p] for a in arrived[q] for s in range(SLOTS)], axis=0) for p in range(2)
            ]
            sums = jnp.dot(place, jnp.concatenate(both, axis=1), preferred_element_type=jnp.float32)
            sums = sums.astype(jnp.bfloat16)
            for n in range(X):
                for p in range(2):
                    outs[n][q, f, p] = sums[n * windows : (n + 1) * windows, p * tile : (p + 1) * tile]


def gram_kernel(places, pos, rows, *refs):
    many = len(places)
    own, theirs, out, held, sems = refs[: many * C], refs[many * C : many * C + many], refs[-3], refs[-2], refs[-1]
    _, bins, _, _, tile = theirs[0].shape
    x, c = pos[2], pos[3]
    count = jnp.int32(0)
    for j in range(rows.shape[1]):
        count += jnp.where(rows[x, j] == x * C + c, 1, 0)
    scale = 1.0 / jnp.full((1, 2 * tile), jnp.maximum(count, 1), jnp.int32).astype(jnp.float32)
    copies = []
    for n, dx in enumerate(places):
        for q in range(C):
            at = n * C + q
            for f in range(bins):
                real, imag = theirs[n][q, f, 0], theirs[n][q, f, 1]
                paired = jnp.concatenate(
                    [jnp.concatenate([real, imag], axis=0), jnp.concatenate([imag, -real], axis=0)], axis=1
                )
                mine = jnp.concatenate([own[at][f, 0], own[at][f, 1]], axis=0)
                gram = lax.dot_general(
                    mine, paired, (((0,), (0,)), ((), ())), preferred_element_type=jnp.float32
                )
                held[at, f] = (gram * scale).astype(jnp.bfloat16)
            place = lax.rem(x - dx + X, X) * C + (c if q == 0 else 1 - c)
            copy = pltpu.make_async_copy(held.at[at], out.at[0, 0, pl.ds(place * bins, bins)], sems.at[at])
            copy.start()
            copies.append(copy)
    for copy in copies:
        copy.wait()


BATCHES = ((0, 1), (3, 2))


def local(spectra, tile_band):
    _, windows, bins, tile = spectra.shape
    grp = lax.axis_index("grp")
    band = lax.axis_index("band")
    bands = X * C
    pos = jnp.stack([grp // Z, grp % Z, band // C, band % C]).astype(jnp.int32)

    row = spread(tile_band).astype(jnp.float32)
    values = spectra.astype(jnp.float32)
    power = jnp.sum(values * values, axis=(0, 2))
    power = power + shift(power, dc=1)
    sent = jnp.concatenate([power, jnp.pad(row, ((0, 7), (0, tile - row.shape[1])))], axis=0)
    crossed = {0: sent}
    for d in (2, 1, 3):
        crossed[d] = shift(sent, dx=d)
    rows = jnp.concatenate([crossed[d][windows : windows + 1, : row.shape[1]] for d in range(X)], axis=0)
    rows = rows.astype(jnp.int32)
    power = sum((crossed[d][:windows] for d in range(1, X)), crossed[0][:windows])
    factor = lax.rsqrt(power / (bins * bands) + 1e-05)
    white = (values * factor[None, :, None, :]).astype(jnp.bfloat16)
    white = jnp.transpose(white, (2, 0, 1, 3))

    ahead = {0: white}
    for d in (2, -2, 1, -1):
        ahead[d] = shift(white, dz=-d)
    ahead[3] = shift(ahead[2], dz=-1)
    ahead[-3] = shift(ahead[-2], dz=1)
    ahead[4] = shift(ahead[2], dz=-2)

    slotted = jax.ShapeDtypeStruct((SLOTS, bins, 2, windows, tile), jnp.bfloat16)
    partial = pl.pallas_call(
        partial_kernel,
        out_shape=[slotted] * Y,
        in_specs=[SMEM] * 2 + [VMEM] * Z,
        out_specs=[VMEM] * Y,
        compiler_params=pltpu.CompilerParams(vmem_limit_bytes=8 << 20),
        name="partial",
    )(pos, rows, *(ahead[d] for d in AHEAD))
    arrived = [shift(partial[d], dy=-d) if d else partial[d] for d in range(Y)]

    own = {(d, 0): shift(white, dx=d) if d else white for d in range(X)}
    for d in range(X):
        own[d, 1] = shift(own[d, 0], dc=1)

    shared = [shift(arrived[d], dc=1) for d in range(Y)]
    partner = pl.pallas_call(
        combine_kernel,
        out_shape=[jax.ShapeDtypeStruct((C, bins, 2, windows, tile), jnp.bfloat16)] * X,
        in_specs=[SMEM] + [VMEM] * (2 * Y),
        out_specs=[VMEM] * X,
        compiler_params=pltpu.CompilerParams(vmem_limit_bytes=8 << 20),
        name="combine",
    )(pos, *arrived, *shared)
    theirs = [shift(partner[d], dx=d) if d else partner[d] for d in range(X)]

    out = None
    for at, places in enumerate(BATCHES):
        operands = [own[d, q] for d in places for q in range(C)] + [theirs[d] for d in places]
        out = pl.pallas_call(
            functools.partial(gram_kernel, places),
            out_shape=jax.ShapeDtypeStruct((1, 1, bands * bins, tile, 2 * tile), jnp.bfloat16),
            in_specs=[SMEM] * 2 + [VMEM] * len(operands) + [ANY] * (at > 0),
            out_specs=ANY,
            scratch_shapes=[
                pltpu.VMEM((len(places) * C, bins, tile, 2 * tile), jnp.bfloat16),
                pltpu.SemaphoreType.DMA((len(places) * C,)),
            ],
            input_output_aliases={2 + len(operands): 0} if at else {},
            compiler_params=pltpu.CompilerParams(vmem_limit_bytes=12 << 20),
        )(pos, rows, *operands, *([out] if at else []))
    return out


def solution(mesh):
    return jax.shard_map(
        local,
        mesh=mesh,
        in_specs=(P(None, None, "band", "grp"), P("grp", None)),
        out_specs=P("grp", "band", None, None, None),
        check_vma=False,
    )
```

```python
import functools

import jax
import jax.numpy as jnp
from jax import lax
from jax.experimental import pallas as pl
from jax.experimental.pallas import tpu as pltpu
from jax.sharding import PartitionSpec as P


Y, Z, X, C = 4, 8, 4, 2
ROWS = ("grp", "band")
SLOTS = 3
AHEAD = (0, 1, 2, 3, 4, -1, -2, -3)
VMEM = pl.BlockSpec(memory_space=pltpu.VMEM)
SMEM = pl.BlockSpec(memory_space=pltpu.SMEM)
ANY = pl.BlockSpec(memory_space=pl.ANY)


def shift(value, dy=0, dz=0, dx=0, dc=0):
    pairs = []
    for y in range(Y):
        for z in range(Z):
            for x in range(X):
                for c in range(C):
                    source = ((y * Z + z) * X + x) * C + c
                    target = (((y + dy) % Y * Z + (z + dz) % Z) * X + (x + dx) % X) * C + (c + dc) % C
                    pairs.append((source, target))
    return lax.ppermute(value, ROWS, pairs)


def first_band(target_row, source_row, z):
    distance = Z * (target_row - source_row) + z
    low = jnp.where(target_row > source_row, distance - (Z - 1), -distance)
    return jnp.where(target_row == source_row, 0, lax.shift_right_arithmetic(low, 2))


def partial_kernel(pos, *refs):
    rows, blocks, outs = refs[0], refs[1 : 1 + Z], refs[1 + Z :]
    bins, _, windows, tile = blocks[0].shape
    y, z = pos[0], pos[1]
    high = SLOTS * windows
    lane = lax.broadcasted_iota(jnp.int32, (high, Z * windows), 1)
    line = lax.broadcasted_iota(jnp.int32, (high, Z * windows), 0)
    same = lane % windows == line % windows
    picks = []
    for d in range(Y):
        first = first_band(lax.rem(y - d + Y, Y), y, z)
        bands = jnp.full((high, Z * windows), -1, jnp.int32)
        for n, off in enumerate(AHEAD):
            bands = jnp.where(lane // windows == n, rows[d, y * Z + lax.rem(z + off + Z, Z)], bands)
        picks.append(jnp.where(same & (bands == first + line // windows), 1.0, 0.0).astype(jnp.bfloat16))
    picks = jnp.concatenate(picks, axis=0)
    for f in range(bins):
        both = [jnp.concatenate([b[f, p] for b in blocks], axis=0) for p in range(2)]
        sums = jnp.dot(picks, jnp.concatenate(both, axis=1), preferred_element_type=jnp.float32)
        sums = sums.astype(jnp.bfloat16)
        for d in range(Y):
            for s in range(SLOTS):
                at = (d * SLOTS + s) * windows
                for p in range(2):
                    outs[d][s, f, p] = sums[at : at + windows, p * tile : (p + 1) * tile]


def combine_kernel(pos, *refs):
    arrived, outs = refs[:Y], refs[Y:]
    _, bins, _, windows, tile = arrived[0].shape
    y, z, x, c = pos[0], pos[1], pos[2], pos[3]
    shape = (X * C * windows, Y * SLOTS * windows)
    lane = lax.broadcasted_iota(jnp.int32, shape, 1)
    line = lax.broadcasted_iota(jnp.int32, shape, 0)
    has = jnp.full(shape, -1, jnp.int32)
    wants = jnp.full(shape, -2, jnp.int32)
    for d in range(Y):
        first = first_band(y, lax.rem(y + d, Y), z)
        for s in range(SLOTS):
            has = jnp.where(lane // windows == d * SLOTS + s, first + s, has)
    for dx in range(X):
        for dc in range(C):
            owner = lax.rem(x + dx, X) * C + lax.rem(c + dc, C)
            wants = jnp.where(line // windows == dx * C + dc, owner, wants)
    place = jnp.where((lane % windows == line % windows) & (has == wants), 1.0, 0.0).astype(jnp.bfloat16)
    for f in range(bins):
        both = [jnp.concatenate([a[s, f, p] for a in arrived for s in range(SLOTS)], axis=0) for p in range(2)]
        sums = jnp.dot(place, jnp.concatenate(both, axis=1), preferred_element_type=jnp.float32)
        sums = sums.astype(jnp.bfloat16)
        for n in range(X * C):
            for p in range(2):
                outs[n][f, p] = sums[n * windows : (n + 1) * windows, p * tile : (p + 1) * tile]


def gram_kernel(places, pos, rows, *refs):
    many = len(places)
    own, theirs, out, held, sems = refs[:many], refs[many : 2 * many], refs[-3], refs[-2], refs[-1]
    bins, _, _, tile = own[0].shape
    x, c = pos[2], pos[3]
    band = x * C + c
    count = jnp.int32(0)
    for j in range(rows.shape[1]):
        count += jnp.where(rows[0, j] == band, 1, 0)
    scale = 1.0 / jnp.full((1, 2 * tile), jnp.maximum(count, 1), jnp.int32).astype(jnp.float32)
    copies = []
    for n, (dx, dc) in enumerate(places):
        for f in range(bins):
            real, imag = theirs[n][f, 0], theirs[n][f, 1]
            paired = jnp.concatenate(
                [jnp.concatenate([real, imag], axis=0), jnp.concatenate([imag, -real], axis=0)], axis=1
            )
            mine = jnp.concatenate([own[n][f, 0], own[n][f, 1]], axis=0)
            gram = lax.dot_general(mine, paired, (((0,), (0,)), ((), ())), preferred_element_type=jnp.float32)
            held[n, f] = (gram * scale).astype(jnp.bfloat16)
        place = lax.rem(x - dx + X, X) * C + lax.rem(c - dc + C, C)
        copy = pltpu.make_async_copy(held.at[n], out.at[0, 0, pl.ds(place * bins, bins)], sems.at[n])
        copy.start()
        copies.append(copy)
    for copy in copies:
        copy.wait()


BATCHES = (((0, 0), (0, 1), (1, 0), (3, 0), (2, 0)), ((2, 1), (1, 1), (3, 1)))


def local(spectra, tile_band):
    _, windows, bins, tile = spectra.shape
    grp = lax.axis_index("grp")
    band = lax.axis_index("band")
    bands = X * C
    pos = jnp.stack([grp // Z, grp % Z, band // C, band % C]).astype(jnp.int32)

    values = spectra.astype(jnp.float32)
    power = jnp.sum(values * values, axis=(0, 2))
    power = power + shift(power, dc=1)
    crossed = [shift(power, dx=d) for d in (2, 1, 3)]
    power = power + crossed[0] + crossed[1] + crossed[2]
    factor = lax.rsqrt(power / (bins * bands) + 1e-05)
    white = (values * factor[None, :, None, :]).astype(jnp.bfloat16)
    white = jnp.transpose(white, (2, 0, 1, 3))

    white, tile_late = lax.optimization_barrier((white, tile_band))
    rows = [tile_band] + [shift(tile_late, dy=d) for d in range(1, Y)]
    rows = jnp.concatenate(rows, axis=0)

    ahead = {0: white}
    for d in (2, -2, 1, -1):
        ahead[d] = shift(white, dz=-d)
    ahead[3] = shift(ahead[2], dz=-1)
    ahead[-3] = shift(ahead[-2], dz=1)
    ahead[4] = shift(ahead[2], dz=-2)

    slotted = jax.ShapeDtypeStruct((SLOTS, bins, 2, windows, tile), jnp.bfloat16)
    partial = pl.pallas_call(
        partial_kernel,
        out_shape=[slotted] * Y,
        in_specs=[SMEM] * 2 + [VMEM] * Z,
        out_specs=[VMEM] * Y,
        compiler_params=pltpu.CompilerParams(vmem_limit_bytes=8 << 20),
        name="partial",
    )(pos, rows, *(ahead[d] for d in AHEAD))
    arrived = [shift(partial[d], dy=-d) if d else partial[d] for d in range(Y)]

    own = {(d, 0): shift(white, dx=d) if d else white for d in range(X)}
    for d in range(X):
        own[d, 1] = shift(own[d, 0], dc=1)

    block = jax.ShapeDtypeStruct((bins, 2, windows, tile), jnp.bfloat16)
    partner = pl.pallas_call(
        combine_kernel,
        out_shape=[block] * bands,
        in_specs=[SMEM] + [VMEM] * Y,
        out_specs=[VMEM] * bands,
        compiler_params=pltpu.CompilerParams(vmem_limit_bytes=8 << 20),
        name="combine",
    )(pos, *arrived)
    theirs = {}
    for dx in range(X):
        for dc in range(C):
            sent = partner[dx * C + dc]
            theirs[dx, dc] = shift(sent, dx=dx, dc=dc) if dx or dc else sent

    out = None
    for at, places in enumerate(BATCHES):
        operands = [own[n] for n in places] + [theirs[n] for n in places]
        out = pl.pallas_call(
            functools.partial(gram_kernel, places),
            out_shape=jax.ShapeDtypeStruct((1, 1, bands * bins, tile, 2 * tile), jnp.bfloat16),
            in_specs=[SMEM] * 2 + [VMEM] * len(operands) + [ANY] * (at > 0),
            out_specs=ANY,
            scratch_shapes=[
                pltpu.VMEM((len(places), bins, tile, 2 * tile), jnp.bfloat16),
                pltpu.SemaphoreType.DMA((len(places),)),
            ],
            input_output_aliases={2 + len(operands): 0} if at else {},
            compiler_params=pltpu.CompilerParams(vmem_limit_bytes=12 << 20),
        )(pos, rows, *operands, *([out] if at else []))
    return out


def solution(mesh):
    return jax.shard_map(
        local,
        mesh=mesh,
        in_specs=(P(None, None, "band", "grp"), P("grp", None)),
        out_specs=P("grp", "band", None, None, None),
        check_vma=False,
    )
```

```python
import functools

import jax
import jax.numpy as jnp
from jax import lax
from jax.experimental import pallas as pl
from jax.experimental.pallas import tpu as pltpu
from jax.sharding import PartitionSpec as P


Y, Z, X, C = 4, 8, 4, 2
ROWS = ("grp", "band")
SLOTS = 3
AHEAD = (0, 1, 2, 3, 4, -1, -2, -3)
VMEM = pl.BlockSpec(memory_space=pltpu.VMEM)
SMEM = pl.BlockSpec(memory_space=pltpu.SMEM)
ANY = pl.BlockSpec(memory_space=pl.ANY)


def shift(value, dy=0, dz=0, dx=0, dc=0):
    pairs = []
    for y in range(Y):
        for z in range(Z):
            for x in range(X):
                for c in range(C):
                    source = ((y * Z + z) * X + x) * C + c
                    target = (((y + dy) % Y * Z + (z + (-dz if c else dz)) % Z) * X + (x + dx) % X) * C + (c + dc) % C
                    pairs.append((source, target))
    return lax.ppermute(value, ROWS, pairs)


def first_band(target_row, source_row, z):
    distance = Z * (target_row - source_row) + z
    low = jnp.where(target_row > source_row, distance - (Z - 1), -distance)
    return jnp.where(target_row == source_row, 0, lax.shift_right_arithmetic(low, 2))


def partial_kernel(pos, *refs):
    rows, blocks, outs = refs[0], refs[1 : 1 + Z], refs[1 + Z :]
    bins, _, windows, tile = blocks[0].shape
    y, z, way = pos[0], pos[1], 1 - 2 * pos[3]
    high = SLOTS * windows
    lane = lax.broadcasted_iota(jnp.int32, (high, Z * windows), 1)
    line = lax.broadcasted_iota(jnp.int32, (high, Z * windows), 0)
    same = lane % windows == line % windows
    picks = []
    for d in range(Y):
        first = first_band(lax.rem(y - d + Y, Y), y, z)
        bands = jnp.full((high, Z * windows), -1, jnp.int32)
        for n, off in enumerate(AHEAD):
            bands = jnp.where(lane // windows == n, rows[d, y * Z + lax.rem(z + way * off + Z, Z)], bands)
        picks.append(jnp.where(same & (bands == first + line // windows), 1.0, 0.0).astype(jnp.bfloat16))
    picks = jnp.concatenate(picks, axis=0)
    for f in range(bins):
        both = [jnp.concatenate([b[f, p] for b in blocks], axis=0) for p in range(2)]
        sums = jnp.dot(picks, jnp.concatenate(both, axis=1), preferred_element_type=jnp.float32)
        sums = sums.astype(jnp.bfloat16)
        for d in range(Y):
            for s in range(SLOTS):
                at = (d * SLOTS + s) * windows
                for p in range(2):
                    outs[d][s, f, p] = sums[at : at + windows, p * tile : (p + 1) * tile]


def combine_kernel(pos, *refs):
    arrived, outs = refs[:Y], refs[Y:]
    _, bins, _, windows, tile = arrived[0].shape
    y, z, x, c = pos[0], pos[1], pos[2], pos[3]
    shape = (X * C * windows, Y * SLOTS * windows)
    lane = lax.broadcasted_iota(jnp.int32, shape, 1)
    line = lax.broadcasted_iota(jnp.int32, shape, 0)
    has = jnp.full(shape, -1, jnp.int32)
    wants = jnp.full(shape, -2, jnp.int32)
    for d in range(Y):
        first = first_band(y, lax.rem(y + d, Y), z)
        for s in range(SLOTS):
            has = jnp.where(lane // windows == d * SLOTS + s, first + s, has)
    for dx in range(X):
        for dc in range(C):
            owner = lax.rem(x + dx, X) * C + lax.rem(c + dc, C)
            wants = jnp.where(line // windows == dx * C + dc, owner, wants)
    place = jnp.where((lane % windows == line % windows) & (has == wants), 1.0, 0.0).astype(jnp.bfloat16)
    for f in range(bins):
        both = [jnp.concatenate([a[s, f, p] for a in arrived for s in range(SLOTS)], axis=0) for p in range(2)]
        sums = jnp.dot(place, jnp.concatenate(both, axis=1), preferred_element_type=jnp.float32)
        sums = sums.astype(jnp.bfloat16)
        for n in range(X * C):
            for p in range(2):
                outs[n][f, p] = sums[n * windows : (n + 1) * windows, p * tile : (p + 1) * tile]


def gram_kernel(places, pos, rows, *refs):
    many = len(places)
    own, theirs, out, held, sems = refs[:many], refs[many : 2 * many], refs[-3], refs[-2], refs[-1]
    bins, _, _, tile = own[0].shape
    x, c = pos[2], pos[3]
    band = x * C + c
    count = jnp.int32(0)
    for j in range(rows.shape[1]):
        count += jnp.where(rows[0, j] == band, 1, 0)
    scale = 1.0 / jnp.full((1, 2 * tile), jnp.maximum(count, 1), jnp.int32).astype(jnp.float32)
    copies = []
    for n, (dx, dc) in enumerate(places):
        for f in range(bins):
            real, imag = theirs[n][f, 0], theirs[n][f, 1]
            paired = jnp.concatenate(
                [jnp.concatenate([real, imag], axis=0), jnp.concatenate([imag, -real], axis=0)], axis=1
            )
            mine = jnp.concatenate([own[n][f, 0], own[n][f, 1]], axis=0)
            gram = lax.dot_general(mine, paired, (((0,), (0,)), ((), ())), preferred_element_type=jnp.float32)
            held[n, f] = (gram * scale).astype(jnp.bfloat16)
        place = lax.rem(x - dx + X, X) * C + lax.rem(c - dc + C, C)
        copy = pltpu.make_async_copy(held.at[n], out.at[0, 0, pl.ds(place * bins, bins)], sems.at[n])
        copy.start()
        copies.append(copy)
    for copy in copies:
        copy.wait()


BATCHES = (((0, 0), (0, 1), (2, 0), (2, 1)), ((1, 0), (1, 1), (3, 0), (3, 1)))


def local(spectra, tile_band):
    _, windows, bins, tile = spectra.shape
    grp = lax.axis_index("grp")
    band = lax.axis_index("band")
    bands = X * C
    pos = jnp.stack([grp // Z, grp % Z, band // C, band % C]).astype(jnp.int32)

    values = spectra.astype(jnp.float32)
    power = jnp.sum(values * values, axis=(0, 2))
    power = power + shift(power, dc=1)
    crossed = [shift(power, dx=d) for d in (2, 1, 3)]
    power = power + crossed[0] + crossed[1] + crossed[2]
    factor = lax.rsqrt(power / (bins * bands) + 1e-05)
    white = (values * factor[None, :, None, :]).astype(jnp.bfloat16)
    white = jnp.transpose(white, (2, 0, 1, 3))

    white, tile_late = lax.optimization_barrier((white, tile_band))
    rows = [tile_band] + [shift(tile_late, dy=d) for d in range(1, Y)]
    rows = jnp.concatenate(rows, axis=0)

    ahead = {0: white}
    for d in (2, -2, 1, -1):
        ahead[d] = shift(white, dz=-d)
    ahead[3] = shift(ahead[2], dz=-1)
    ahead[-3] = shift(ahead[-2], dz=1)
    ahead[4] = shift(ahead[2], dz=-2)

    slotted = jax.ShapeDtypeStruct((SLOTS, bins, 2, windows, tile), jnp.bfloat16)
    partial = pl.pallas_call(
        partial_kernel,
        out_shape=[slotted] * Y,
        in_specs=[SMEM] * 2 + [VMEM] * Z,
        out_specs=[VMEM] * Y,
        compiler_params=pltpu.CompilerParams(vmem_limit_bytes=8 << 20),
        name="partial",
    )(pos, rows, *(ahead[d] for d in AHEAD))
    arrived = [shift(partial[d], dy=-d) if d else partial[d] for d in range(Y)]

    own = {(d, 0): shift(white, dx=d) if d else white for d in range(X)}
    for d in range(X):
        own[d, 1] = shift(own[d, 0], dc=1)

    block = jax.ShapeDtypeStruct((bins, 2, windows, tile), jnp.bfloat16)
    partner = pl.pallas_call(
        combine_kernel,
        out_shape=[block] * bands,
        in_specs=[SMEM] + [VMEM] * Y,
        out_specs=[VMEM] * bands,
        compiler_params=pltpu.CompilerParams(vmem_limit_bytes=8 << 20),
        name="combine",
    )(pos, *arrived)
    theirs = {}
    for dx in range(X):
        for dc in range(C):
            sent = partner[dx * C + dc]
            theirs[dx, dc] = shift(sent, dx=dx, dc=dc) if dx or dc else sent

    out = None
    for at, places in enumerate(BATCHES):
        operands = [own[n] for n in places] + [theirs[n] for n in places]
        out = pl.pallas_call(
            functools.partial(gram_kernel, places),
            out_shape=jax.ShapeDtypeStruct((1, 1, bands * bins, tile, 2 * tile), jnp.bfloat16),
            in_specs=[SMEM] * 2 + [VMEM] * len(operands) + [ANY] * (at > 0),
            out_specs=ANY,
            scratch_shapes=[
                pltpu.VMEM((len(places), bins, tile, 2 * tile), jnp.bfloat16),
                pltpu.SemaphoreType.DMA((len(places),)),
            ],
            input_output_aliases={2 + len(operands): 0} if at else {},
            compiler_params=pltpu.CompilerParams(vmem_limit_bytes=12 << 20),
        )(pos, rows, *operands, *([out] if at else []))
    return out


def solution(mesh):
    return jax.shard_map(
        local,
        mesh=mesh,
        in_specs=(P(None, None, "band", "grp"), P("grp", None)),
        out_specs=P("grp", "band", None, None, None),
        check_vma=False,
    )
```

```python
import functools

import jax
import jax.numpy as jnp
from jax import lax
from jax.experimental import pallas as pl
from jax.experimental.pallas import tpu as pltpu
from jax.sharding import PartitionSpec as P


Y, Z, X, C = 4, 8, 4, 2
ROWS = ("grp", "band")
SLOTS = 3
AHEAD = (0, 1, 2, 3, 4, -1, -2, -3)
VMEM = pl.BlockSpec(memory_space=pltpu.VMEM)
SMEM = pl.BlockSpec(memory_space=pltpu.SMEM)
ANY = pl.BlockSpec(memory_space=pl.ANY)


def shift(value, dy=0, dz=0, dx=0, dc=0, turn=0):
    pairs = []
    for y in range(Y):
        for z in range(Z):
            for x in range(X):
                for c in range(C):
                    source = ((y * Z + z) * X + x) * C + c
                    target = (((y + dy + (-turn if c else turn)) % Y * Z + (z + (-dz if c else dz)) % Z) * X + (x + dx) % X) * C + (c + dc) % C
                    pairs.append((source, target))
    return lax.ppermute(value, ROWS, pairs)


def first_band(target_row, source_row, z):
    distance = Z * (target_row - source_row) + z
    low = jnp.where(target_row > source_row, distance - (Z - 1), -distance)
    return jnp.where(target_row == source_row, 0, lax.shift_right_arithmetic(low, 2))


def partial_kernel(pos, *refs):
    rows, blocks, outs = refs[0], refs[1 : 1 + Z], refs[1 + Z :]
    bins, _, windows, tile = blocks[0].shape
    y, z, way = pos[0], pos[1], 1 - 2 * pos[3]
    high = SLOTS * windows
    lane = lax.broadcasted_iota(jnp.int32, (high, Z * windows), 1)
    line = lax.broadcasted_iota(jnp.int32, (high, Z * windows), 0)
    same = lane % windows == line % windows
    picks = []
    for d in range(Y):
        first = first_band(lax.rem(y - d + Y, Y), y, z)
        bands = jnp.full((high, Z * windows), -1, jnp.int32)
        for n, off in enumerate(AHEAD):
            bands = jnp.where(lane // windows == n, rows[d, y * Z + lax.rem(z + way * off + Z, Z)], bands)
        picks.append(jnp.where(same & (bands == first + line // windows), 1.0, 0.0).astype(jnp.bfloat16))
    picks = jnp.concatenate(picks, axis=0)
    for f in range(bins):
        both = [jnp.concatenate([b[f, p] for b in blocks], axis=0) for p in range(2)]
        sums = jnp.dot(picks, jnp.concatenate(both, axis=1), preferred_element_type=jnp.float32)
        sums = sums.astype(jnp.bfloat16)
        for d in range(Y):
            for s in range(SLOTS):
                at = (d * SLOTS + s) * windows
                for p in range(2):
                    outs[d][s, f, p] = sums[at : at + windows, p * tile : (p + 1) * tile]


def combine_kernel(pos, *refs):
    arrived, outs = refs[:Y], refs[Y:]
    _, bins, _, windows, tile = arrived[0].shape
    y, z, x, c = pos[0], pos[1], pos[2], pos[3]
    shape = (X * C * windows, Y * SLOTS * windows)
    lane = lax.broadcasted_iota(jnp.int32, shape, 1)
    line = lax.broadcasted_iota(jnp.int32, shape, 0)
    has = jnp.full(shape, -1, jnp.int32)
    wants = jnp.full(shape, -2, jnp.int32)
    for d in range(Y):
        first = first_band(y, lax.rem(y + d, Y), z)
        for s in range(SLOTS):
            has = jnp.where(lane // windows == d * SLOTS + s, first + s, has)
    for dx in range(X):
        for dc in range(C):
            owner = lax.rem(x + dx, X) * C + lax.rem(c + dc, C)
            wants = jnp.where(line // windows == dx * C + dc, owner, wants)
    place = jnp.where((lane % windows == line % windows) & (has == wants), 1.0, 0.0).astype(jnp.bfloat16)
    for f in range(bins):
        both = [jnp.concatenate([a[s, f, p] for a in arrived for s in range(SLOTS)], axis=0) for p in range(2)]
        sums = jnp.dot(place, jnp.concatenate(both, axis=1), preferred_element_type=jnp.float32)
        sums = sums.astype(jnp.bfloat16)
        for n in range(X * C):
            for p in range(2):
                outs[n][f, p] = sums[n * windows : (n + 1) * windows, p * tile : (p + 1) * tile]


def gram_kernel(places, pos, rows, *refs):
    many = len(places)
    own, theirs, out, held, sems = refs[:many], refs[many : 2 * many], refs[-3], refs[-2], refs[-1]
    bins, _, _, tile = own[0].shape
    x, c = pos[2], pos[3]
    band = x * C + c
    count = jnp.int32(0)
    for j in range(rows.shape[1]):
        count += jnp.where(rows[0, j] == band, 1, 0)
    scale = 1.0 / jnp.full((1, 2 * tile), jnp.maximum(count, 1), jnp.int32).astype(jnp.float32)
    copies = []
    for n, (dx, dc) in enumerate(places):
        for f in range(bins):
            real, imag = theirs[n][f, 0], theirs[n][f, 1]
            paired = jnp.concatenate(
                [jnp.concatenate([real, imag], axis=0), jnp.concatenate([imag, -real], axis=0)], axis=1
            )
            mine = jnp.concatenate([own[n][f, 0], own[n][f, 1]], axis=0)
            gram = lax.dot_general(mine, paired, (((0,), (0,)), ((), ())), preferred_element_type=jnp.float32)
            held[n, f] = (gram * scale).astype(jnp.bfloat16)
        place = lax.rem(x - dx + X, X) * C + lax.rem(c - dc + C, C)
        copy = pltpu.make_async_copy(held.at[n], out.at[0, 0, pl.ds(place * bins, bins)], sems.at[n])
        copy.start()
        copies.append(copy)
    for copy in copies:
        copy.wait()


BATCHES = (((0, 0), (0, 1), (2, 0), (2, 1)), ((1, 0), (1, 1), (3, 0), (3, 1)))


def local(spectra, tile_band):
    _, windows, bins, tile = spectra.shape
    grp = lax.axis_index("grp")
    band = lax.axis_index("band")
    bands = X * C
    pos = jnp.stack([grp // Z, grp % Z, band // C, band % C]).astype(jnp.int32)

    values = spectra.astype(jnp.float32)
    power = jnp.sum(values * values, axis=(0, 2))
    power = power + shift(power, dc=1)
    crossed = [shift(power, dx=d) for d in (2, 1, 3)]
    power = power + crossed[0] + crossed[1] + crossed[2]
    factor = lax.rsqrt(power / (bins * bands) + 1e-05)
    white = (values * factor[None, :, None, :]).astype(jnp.bfloat16)
    white = jnp.transpose(white, (2, 0, 1, 3))

    white, tile_late = lax.optimization_barrier((white, tile_band))
    rows = [tile_band] + [shift(tile_late, dy=d) for d in range(1, Y)]
    rows = jnp.concatenate(rows, axis=0)

    ahead = {0: white}
    for d in (2, -2, 1, -1):
        ahead[d] = shift(white, dz=-d)
    ahead[3] = shift(ahead[2], dz=-1)
    ahead[-3] = shift(ahead[-2], dz=1)
    ahead[4] = shift(ahead[2], dz=-2)

    slotted = jax.ShapeDtypeStruct((SLOTS, bins, 2, windows, tile), jnp.bfloat16)
    partial = pl.pallas_call(
        partial_kernel,
        out_shape=[slotted] * Y,
        in_specs=[SMEM] * 2 + [VMEM] * Z,
        out_specs=[VMEM] * Y,
        compiler_params=pltpu.CompilerParams(vmem_limit_bytes=8 << 20),
        name="partial",
    )(pos, rows, *(ahead[d] for d in AHEAD))
    passed = shift(partial[2], turn=1)
    arrived = [partial[0], None, shift(passed, turn=1), None]
    for d in (1, 3):
        arrived[d] = shift(partial[d], dy=-d)

    own = {(d, 0): shift(white, dx=d) if d else white for d in range(X)}
    for d in range(X):
        own[d, 1] = shift(own[d, 0], dc=1)

    block = jax.ShapeDtypeStruct((bins, 2, windows, tile), jnp.bfloat16)
    partner = pl.pallas_call(
        combine_kernel,
        out_shape=[block] * bands,
        in_specs=[SMEM] + [VMEM] * Y,
        out_specs=[VMEM] * bands,
        compiler_params=pltpu.CompilerParams(vmem_limit_bytes=8 << 20),
        name="combine",
    )(pos, *arrived)
    theirs = {}
    for dx in range(X):
        for dc in range(C):
            sent = partner[dx * C + dc]
            theirs[dx, dc] = shift(sent, dx=dx, dc=dc) if dx or dc else sent

    out = None
    for at, places in enumerate(BATCHES):
        operands = [own[n] for n in places] + [theirs[n] for n in places]
        out = pl.pallas_call(
            functools.partial(gram_kernel, places),
            out_shape=jax.ShapeDtypeStruct((1, 1, bands * bins, tile, 2 * tile), jnp.bfloat16),
            in_specs=[SMEM] * 2 + [VMEM] * len(operands) + [ANY] * (at > 0),
            out_specs=ANY,
            scratch_shapes=[
                pltpu.VMEM((len(places), bins, tile, 2 * tile), jnp.bfloat16),
                pltpu.SemaphoreType.DMA((len(places),)),
            ],
            input_output_aliases={2 + len(operands): 0} if at else {},
            compiler_params=pltpu.CompilerParams(vmem_limit_bytes=12 << 20),
        )(pos, rows, *operands, *([out] if at else []))
    return out


def solution(mesh):
    return jax.shard_map(
        local,
        mesh=mesh,
        in_specs=(P(None, None, "band", "grp"), P("grp", None)),
        out_specs=P("grp", "band", None, None, None),
        check_vma=False,
    )
```

```python
import functools

import jax
import jax.numpy as jnp
from jax import lax
from jax.experimental import pallas as pl
from jax.experimental.pallas import tpu as pltpu
from jax.sharding import PartitionSpec as P


Y, Z, X, C = 4, 8, 4, 2
ROWS = ("grp", "band")
SLOTS = 3
AHEAD = (0, 1, 2, 3, 4, -1, -2, -3)
VMEM = pl.BlockSpec(memory_space=pltpu.VMEM)
SMEM = pl.BlockSpec(memory_space=pltpu.SMEM)
ANY = pl.BlockSpec(memory_space=pl.ANY)


def shift(value, dy=0, dz=0, dx=0, dc=0):
    pairs = []
    for y in range(Y):
        for z in range(Z):
            for x in range(X):
                for c in range(C):
                    source = ((y * Z + z) * X + x) * C + c
                    target = (((y + dy) % Y * Z + (z + dz) % Z) * X + (x + dx) % X) * C + (c + dc) % C
                    pairs.append((source, target))
    return lax.ppermute(value, ROWS, pairs)


def first_band(target_row, source_row, z):
    distance = Z * (target_row - source_row) + z
    low = jnp.where(target_row > source_row, distance - (Z - 1), -distance)
    return jnp.where(target_row == source_row, 0, lax.shift_right_arithmetic(low, 2))


def partial_kernel(pos, *refs):
    rows, blocks, outs = refs[0], refs[1 : 1 + Z], refs[1 + Z :]
    bins, _, windows, tile = blocks[0].shape
    y, z = pos[0], pos[1]
    high = SLOTS * windows
    lane = lax.broadcasted_iota(jnp.int32, (high, Z * windows), 1)
    line = lax.broadcasted_iota(jnp.int32, (high, Z * windows), 0)
    same = lane % windows == line % windows
    picks = []
    for d in range(Y):
        first = first_band(lax.rem(y - d + Y, Y), y, z)
        bands = jnp.full((high, Z * windows), -1, jnp.int32)
        for n, off in enumerate(AHEAD):
            bands = jnp.where(lane // windows == n, rows[d, y * Z + lax.rem(z + off + Z, Z)], bands)
        picks.append(jnp.where(same & (bands == first + line // windows), 1.0, 0.0).astype(jnp.bfloat16))
    picks = jnp.concatenate(picks, axis=0)
    for f in range(bins):
        both = [jnp.concatenate([b[f, p] for b in blocks], axis=0) for p in range(2)]
        sums = jnp.dot(picks, jnp.concatenate(both, axis=1), preferred_element_type=jnp.float32)
        sums = sums.astype(jnp.bfloat16)
        for d in range(Y):
            for s in range(SLOTS):
                at = (d * SLOTS + s) * windows
                for p in range(2):
                    outs[d][s, f, p] = sums[at : at + windows, p * tile : (p + 1) * tile]


def place_kernel(pos, out):
    y, z, x, c = pos[0], pos[1], pos[2], pos[3]
    windows = out.shape[0] // (X * C)
    lane = lax.broadcasted_iota(jnp.int32, out.shape, 1)
    line = lax.broadcasted_iota(jnp.int32, out.shape, 0)
    has = jnp.full(out.shape, -1, jnp.int32)
    wants = jnp.full(out.shape, -2, jnp.int32)
    for d in range(Y):
        first = first_band(y, lax.rem(y + d, Y), z)
        for s in range(SLOTS):
            has = jnp.where(lane // windows == d * SLOTS + s, first + s, has)
    for dx in range(X):
        for dc in range(C):
            owner = lax.rem(x + dx, X) * C + lax.rem(c + dc, C)
            wants = jnp.where(line // windows == dx * C + dc, owner, wants)
    out[...] = jnp.where((lane % windows == line % windows) & (has == wants), 1.0, 0.0).astype(jnp.bfloat16)


def combine_kernel(place, *refs):
    arrived, outs = refs[:Y], refs[Y:]
    _, bins, _, windows, tile = arrived[0].shape
    for f in range(bins):
        both = [jnp.concatenate([a[s, f, p] for a in arrived for s in range(SLOTS)], axis=0) for p in range(2)]
        sums = jnp.dot(place[...], jnp.concatenate(both, axis=1), preferred_element_type=jnp.float32)
        sums = sums.astype(jnp.bfloat16)
        for n in range(X * C):
            for p in range(2):
                outs[n][f, p] = sums[n * windows : (n + 1) * windows, p * tile : (p + 1) * tile]


def gram_kernel(places, pos, rows, *refs):
    many = len(places)
    own, theirs, out, held, sems = refs[:many], refs[many : 2 * many], refs[-3], refs[-2], refs[-1]
    bins, _, _, tile = own[0].shape
    x, c = pos[2], pos[3]
    band = x * C + c
    count = jnp.int32(0)
    for j in range(rows.shape[1]):
        count += jnp.where(rows[0, j] == band, 1, 0)
    scale = 1.0 / jnp.full((1, 2 * tile), jnp.maximum(count, 1), jnp.int32).astype(jnp.float32)
    copies = []
    for n, (dx, dc) in enumerate(places):
        place = lax.rem(x - dx + X, X) * C + lax.rem(c - dc + C, C)
        for f in range(bins):
            real, imag = theirs[n][f, 0], theirs[n][f, 1]
            paired = jnp.concatenate(
                [jnp.concatenate([real, imag], axis=0), jnp.concatenate([imag, -real], axis=0)], axis=1
            )
            mine = jnp.concatenate([own[n][f, 0], own[n][f, 1]], axis=0)
            gram = lax.dot_general(mine, paired, (((0,), (0,)), ((), ())), preferred_element_type=jnp.float32)
            held[n, f] = (gram * scale).astype(jnp.bfloat16)
            if f % 2:
                copy = pltpu.make_async_copy(
                    held.at[n, pl.ds(f - 1, 2)],
                    out.at[0, 0, pl.ds(place * bins + f - 1, 2)],
                    sems.at[n * (bins // 2) + f // 2],
                )
                copy.start()
                copies.append(copy)
    for copy in copies:
        copy.wait()


BATCHES = (((0, 0), (0, 1), (2, 0), (2, 1)), ((1, 0), (1, 1), (3, 0), (3, 1)))


def local(spectra, tile_band):
    _, windows, bins, tile = spectra.shape
    grp = lax.axis_index("grp")
    band = lax.axis_index("band")
    bands = X * C
    pos = jnp.stack([grp // Z, grp % Z, band // C, band % C]).astype(jnp.int32)

    values = spectra.astype(jnp.float32)
    power = jnp.sum(values * values, axis=(0, 2))
    power = power + shift(power, dc=1)
    crossed = [shift(power, dx=d) for d in (2, 1, 3)]
    power = power + crossed[0] + crossed[1] + crossed[2]
    factor = lax.rsqrt(power / (bins * bands) + 1e-05)
    white = (values * factor[None, :, None, :]).astype(jnp.bfloat16)
    white = jnp.transpose(white, (2, 0, 1, 3))

    white, tile_late = lax.optimization_barrier((white, tile_band))
    rows = [tile_band] + [shift(tile_late, dy=d) for d in range(1, Y)]
    rows = jnp.concatenate(rows, axis=0)

    ahead = {0: white}
    for d in (2, -2, 1, -1):
        ahead[d] = shift(white, dz=-d)
    ahead[3] = shift(ahead[2], dz=-1)
    ahead[-3] = shift(ahead[-2], dz=1)
    ahead[4] = shift(ahead[2], dz=-2)

    slotted = jax.ShapeDtypeStruct((SLOTS, bins, 2, windows, tile), jnp.bfloat16)
    partial = pl.pallas_call(
        partial_kernel,
        out_shape=[slotted] * Y,
        in_specs=[SMEM] * 2 + [VMEM] * Z,
        out_specs=[VMEM] * Y,
        compiler_params=pltpu.CompilerParams(vmem_limit_bytes=8 << 20),
        name="partial",
    )(pos, rows, *(ahead[d] for d in AHEAD))
    arrived = [shift(partial[d], dy=-d) if d else partial[d] for d in range(Y)]

    own = {(d, 0): shift(white, dx=d) if d else white for d in range(X)}
    for d in range(X):
        own[d, 1] = shift(own[d, 0], dc=1)

    place = pl.pallas_call(
        place_kernel,
        out_shape=jax.ShapeDtypeStruct((bands * windows, Y * SLOTS * windows), jnp.bfloat16),
        in_specs=[SMEM],
        out_specs=VMEM,
        compiler_params=pltpu.CompilerParams(vmem_limit_bytes=4 << 20),
        name="place",
    )(pos)
    block = jax.ShapeDtypeStruct((bins, 2, windows, tile), jnp.bfloat16)
    partner = pl.pallas_call(
        combine_kernel,
        out_shape=[block] * bands,
        in_specs=[VMEM] * (1 + Y),
        out_specs=[VMEM] * bands,
        compiler_params=pltpu.CompilerParams(vmem_limit_bytes=8 << 20),
        name="combine",
    )(place, *arrived)
    theirs = {}
    for dx in range(X):
        for dc in range(C):
            sent = partner[dx * C + dc]
            theirs[dx, dc] = shift(sent, dx=dx, dc=dc) if dx or dc else sent

    out = None
    for at, places in enumerate(BATCHES):
        operands = [own[n] for n in places] + [theirs[n] for n in places]
        out = pl.pallas_call(
            functools.partial(gram_kernel, places),
            out_shape=jax.ShapeDtypeStruct((1, 1, bands * bins, tile, 2 * tile), jnp.bfloat16),
            in_specs=[SMEM] * 2 + [VMEM] * len(operands) + [ANY] * (at > 0),
            out_specs=ANY,
            scratch_shapes=[
                pltpu.VMEM((len(places), bins, tile, 2 * tile), jnp.bfloat16),
                pltpu.SemaphoreType.DMA((len(places) * bins // 2,)),
            ],
            input_output_aliases={2 + len(operands): 0} if at else {},
            compiler_params=pltpu.CompilerParams(vmem_limit_bytes=12 << 20),
        )(pos, rows, *operands, *([out] if at else []))
    return out


def solution(mesh):
    return jax.shard_map(
        local,
        mesh=mesh,
        in_specs=(P(None, None, "band", "grp"), P("grp", None)),
        out_specs=P("grp", "band", None, None, None),
        check_vma=False,
    )
```

```python
import functools

import jax
import jax.numpy as jnp
from jax import lax
from jax.experimental import pallas as pl
from jax.experimental.pallas import tpu as pltpu
from jax.sharding import PartitionSpec as P


Y, Z, X, C = 4, 8, 4, 2
ROWS = ("grp", "band")
SLOTS = 3
AHEAD = (0, 1, 2, 3, 4, -1, -2, -3)
VMEM = pl.BlockSpec(memory_space=pltpu.VMEM)
SMEM = pl.BlockSpec(memory_space=pltpu.SMEM)
ANY = pl.BlockSpec(memory_space=pl.ANY)


def shift(value, dy=0, dz=0, dx=0, dc=0):
    pairs = []
    for y in range(Y):
        for z in range(Z):
            for x in range(X):
                for c in range(C):
                    source = ((y * Z + z) * X + x) * C + c
                    target = (((y + dy) % Y * Z + (z + (-dz if c else dz)) % Z) * X + (x + dx) % X) * C + (c + dc) % C
                    pairs.append((source, target))
    return lax.ppermute(value, ROWS, pairs)


def first_band(target_row, source_row, z):
    distance = Z * (target_row - source_row) + z
    low = jnp.where(target_row > source_row, distance - (Z - 1), -distance)
    return jnp.where(target_row == source_row, 0, lax.shift_right_arithmetic(low, 2))


def partial_kernel(pos, *refs):
    rows, blocks, outs = refs[0], refs[1 : 1 + Z], refs[1 + Z :]
    bins, _, windows, tile = blocks[0].shape
    y, z, way = pos[0], pos[1], 1 - 2 * pos[3]
    high = SLOTS * windows
    lane = lax.broadcasted_iota(jnp.int32, (high, Z * windows), 1)
    line = lax.broadcasted_iota(jnp.int32, (high, Z * windows), 0)
    same = lane % windows == line % windows
    picks = []
    for d in range(Y):
        first = first_band(lax.rem(y - d + Y, Y), y, z)
        bands = jnp.full((high, Z * windows), -1, jnp.int32)
        for n, off in enumerate(AHEAD):
            bands = jnp.where(lane // windows == n, rows[d, y * Z + lax.rem(z + way * off + Z, Z)], bands)
        picks.append(jnp.where(same & (bands == first + line // windows), 1.0, 0.0).astype(jnp.bfloat16))
    picks = jnp.concatenate(picks, axis=0)
    for f in range(bins):
        both = [jnp.concatenate([b[f, p] for b in blocks], axis=0) for p in range(2)]
        sums = jnp.dot(picks, jnp.concatenate(both, axis=1), preferred_element_type=jnp.float32)
        sums = sums.astype(jnp.bfloat16)
        for d in range(Y):
            for s in range(SLOTS):
                at = (d * SLOTS + s) * windows
                for p in range(2):
                    outs[d][s, f, p] = sums[at : at + windows, p * tile : (p + 1) * tile]


def place_kernel(pos, out):
    y, z, x, c = pos[0], pos[1], pos[2], pos[3]
    windows = out.shape[0] // (X * C)
    lane = lax.broadcasted_iota(jnp.int32, out.shape, 1)
    line = lax.broadcasted_iota(jnp.int32, out.shape, 0)
    has = jnp.full(out.shape, -1, jnp.int32)
    wants = jnp.full(out.shape, -2, jnp.int32)
    for d in range(Y):
        first = first_band(y, lax.rem(y + d, Y), z)
        for s in range(SLOTS):
            has = jnp.where(lane // windows == d * SLOTS + s, first + s, has)
    for dx in range(X):
        for dc in range(C):
            owner = lax.rem(x + dx, X) * C + lax.rem(c + dc, C)
            wants = jnp.where(line // windows == dx * C + dc, owner, wants)
    out[...] = jnp.where((lane % windows == line % windows) & (has == wants), 1.0, 0.0).astype(jnp.bfloat16)


def combine_kernel(place, *refs):
    arrived, outs = refs[:Y], refs[Y:]
    _, bins, _, windows, tile = arrived[0].shape
    for f in range(bins):
        both = [jnp.concatenate([a[s, f, p] for a in arrived for s in range(SLOTS)], axis=0) for p in range(2)]
        sums = jnp.dot(place[...], jnp.concatenate(both, axis=1), preferred_element_type=jnp.float32)
        sums = sums.astype(jnp.bfloat16)
        for n in range(X * C):
            for p in range(2):
                outs[n][f, p] = sums[n * windows : (n + 1) * windows, p * tile : (p + 1) * tile]


def gram_kernel(places, pos, rows, *refs):
    many = len(places)
    own, theirs, out, held, sems = refs[:many], refs[many : 2 * many], refs[-3], refs[-2], refs[-1]
    bins, _, _, tile = own[0].shape
    x, c = pos[2], pos[3]
    band = x * C + c
    count = jnp.int32(0)
    for j in range(rows.shape[1]):
        count += jnp.where(rows[0, j] == band, 1, 0)
    scale = 1.0 / jnp.full((1, 2 * tile), jnp.maximum(count, 1), jnp.int32).astype(jnp.float32)
    copies = []
    for n, (dx, dc) in enumerate(places):
        place = lax.rem(x - dx + X, X) * C + lax.rem(c - dc + C, C)
        for f in range(bins):
            real, imag = theirs[n][f, 0], theirs[n][f, 1]
            paired = jnp.concatenate(
                [jnp.concatenate([real, imag], axis=0), jnp.concatenate([imag, -real], axis=0)], axis=1
            )
            mine = jnp.concatenate([own[n][f, 0], own[n][f, 1]], axis=0)
            gram = lax.dot_general(mine, paired, (((0,), (0,)), ((), ())), preferred_element_type=jnp.float32)
            held[n, f] = (gram * scale).astype(jnp.bfloat16)
            if f % 2:
                copy = pltpu.make_async_copy(
                    held.at[n, pl.ds(f - 1, 2)],
                    out.at[0, 0, pl.ds(place * bins + f - 1, 2)],
                    sems.at[n * (bins // 2) + f // 2],
                )
                copy.start()
                copies.append(copy)
    for copy in copies:
        copy.wait()


BATCHES = (((0, 0), (0, 1), (2, 0), (2, 1), (1, 0)), ((1, 1), (3, 0), (3, 1)))


def local(spectra, tile_band):
    _, windows, bins, tile = spectra.shape
    grp = lax.axis_index("grp")
    band = lax.axis_index("band")
    bands = X * C
    pos = jnp.stack([grp // Z, grp % Z, band // C, band % C]).astype(jnp.int32)

    values = spectra.astype(jnp.float32)
    power = jnp.sum(values * values, axis=(0, 2))
    power = power + shift(power, dc=1)
    crossed = [shift(power, dx=d) for d in (2, 1, 3)]
    power = power + crossed[0] + crossed[1] + crossed[2]
    factor = lax.rsqrt(power / (bins * bands) + 1e-05)
    white = (values * factor[None, :, None, :]).astype(jnp.bfloat16)
    white = jnp.transpose(white, (2, 0, 1, 3))

    white, tile_late = lax.optimization_barrier((white, tile_band))
    rows = [tile_band] + [shift(tile_late, dy=d) for d in range(1, Y)]
    rows = jnp.concatenate(rows, axis=0)

    ahead = {0: white}
    for d in (2, -2, 1, -1):
        ahead[d] = shift(white, dz=-d)
    ahead[3] = shift(ahead[2], dz=-1)
    ahead[-3] = shift(ahead[-2], dz=1)
    ahead[4] = shift(ahead[2], dz=-2)

    slotted = jax.ShapeDtypeStruct((SLOTS, bins, 2, windows, tile), jnp.bfloat16)
    partial = pl.pallas_call(
        partial_kernel,
        out_shape=[slotted] * Y,
        in_specs=[SMEM] * 2 + [VMEM] * Z,
        out_specs=[VMEM] * Y,
        compiler_params=pltpu.CompilerParams(vmem_limit_bytes=8 << 20),
        name="partial",
    )(pos, rows, *(ahead[d] for d in AHEAD))
    arrived = [shift(partial[d], dy=-d) if d else partial[d] for d in range(Y)]

    own = {(d, 0): shift(white, dx=d) if d else white for d in range(X)}
    for d in range(X):
        own[d, 1] = shift(own[d, 0], dc=1)

    place = pl.pallas_call(
        place_kernel,
        out_shape=jax.ShapeDtypeStruct((bands * windows, Y * SLOTS * windows), jnp.bfloat16),
        in_specs=[SMEM],
        out_specs=VMEM,
        compiler_params=pltpu.CompilerParams(vmem_limit_bytes=4 << 20),
        name="place",
    )(pos)
    block = jax.ShapeDtypeStruct((bins, 2, windows, tile), jnp.bfloat16)
    partner = pl.pallas_call(
        combine_kernel,
        out_shape=[block] * bands,
        in_specs=[VMEM] * (1 + Y),
        out_specs=[VMEM] * bands,
        compiler_params=pltpu.CompilerParams(vmem_limit_bytes=8 << 20),
        name="combine",
    )(place, *arrived)
    theirs = {}
    for dx in range(X):
        for dc in range(C):
            sent = partner[dx * C + dc]
            theirs[dx, dc] = shift(sent, dx=dx, dc=dc) if dx or dc else sent

    out = None
    for at, places in enumerate(BATCHES):
        operands = [own[n] for n in places] + [theirs[n] for n in places]
        out = pl.pallas_call(
            functools.partial(gram_kernel, places),
            out_shape=jax.ShapeDtypeStruct((1, 1, bands * bins, tile, 2 * tile), jnp.bfloat16),
            in_specs=[SMEM] * 2 + [VMEM] * len(operands) + [ANY] * (at > 0),
            out_specs=ANY,
            scratch_shapes=[
                pltpu.VMEM((len(places), bins, tile, 2 * tile), jnp.bfloat16),
                pltpu.SemaphoreType.DMA((len(places) * bins // 2,)),
            ],
            input_output_aliases={2 + len(operands): 0} if at else {},
            compiler_params=pltpu.CompilerParams(vmem_limit_bytes=12 << 20),
        )(pos, rows, *operands, *([out] if at else []))
    return out


def solution(mesh):
    return jax.shard_map(
        local,
        mesh=mesh,
        in_specs=(P(None, None, "band", "grp"), P("grp", None)),
        out_specs=P("grp", "band", None, None, None),
        check_vma=False,
    )
```
